512 devices in a mesh: grow: 64 (over y, z_lo, core), trans: 8 (over z_hi, x).
Axes of the slice: x: 4, y: 8, z: 8 (z_hi: 2, z_lo: 4; z = z_hi * 4 + z_lo), core: 2. Of those that a mesh axis runs over, the one named last changes fastest.
Arguments:
- phase_label: int32 [1536, 64, 128], P('grow', 'trans'), may hold values from 0 to 3
- grain_label: int32 [1536, 64, 128], P('grow', 'trans'), may hold values from 0 to 31
- grain_orient: int32 [32], replicated, may hold values from 0 to 7
- orient_mobility: float32 [8], replicated, may hold values from 0.4 to 1.2
- solute_init: float32 [2, 1536, 64, 128], P(None, 'grow', 'trans'), may hold values from 0.1 to 0.5
- partition: float32 [4, 2], replicated, may hold values from -0.5 to 0.5
Outputs:
- phase_out: float32 [4, 1536, 64, 128], P(None, 'grow', 'trans')
- solute_out: float32 [2, 1536, 64, 128], P(None, 'grow', 'trans')
The draws below stay inside these ranges and needn't reach their ends.
All inputs are finite; a program needn't handle non-finite values.
Results may differ from the reference program's by a relative error of at most 0.00002.
Values sent between devices are 32-bit elements; how exact they have to be, the bound alone decides.
A program may use at most 64 MiB of HBM per device.

```python
import math
import jax
import jax.numpy as jnp

COLUMNS = 128
SHIFT = 16
PHASES = 4
SOLUTES = 2
GRAINS = 32
ORIENTS = 8
DEPTH = 1536
BREADTH = 64


def touch_ends(entries, own_key, least, top_value):
    longest = entries.shape.index(max(entries.shape))
    spots = []
    for shift in (0, 1):
        where = [jax.random.randint(jax.random.fold_in(own_key, axis), (), 0, length) for axis, length in enumerate(entries.shape)]
        where[longest] = (where[longest] + shift) % entries.shape[longest]
        spots.append(tuple(where))
    return entries.at[spots[0]].set(least).at[spots[1]].set(top_value)


def steps_of(own_key, shape, cuts, low, largest):
    loudness, own = 1.0, jax.random.fold_in(own_key, 6)
    for position, parts in cuts:
        steps = jnp.exp(jax.random.uniform(jax.random.fold_in(own, position), (parts,), jnp.float32, low / len(cuts), largest / len(cuts)))
        loudness = loudness * jnp.repeat(steps, shape[position] // parts).reshape([-1 if axis == position else 1 for axis in range(len(shape))])
    return loudness


def setup_inputs(seed: int = 0) -> dict:
    arg_keys = jax.random.split(jax.random.key(seed), 7)
    phase_label = touch_ends(jax.random.randint(arg_keys[0], (DEPTH, BREADTH, COLUMNS), 0, PHASES), jax.random.fold_in(arg_keys[0], 1), 0, PHASES - 1).astype(jnp.int32)
    grain_label = touch_ends(jax.random.randint(arg_keys[1], (DEPTH, BREADTH, COLUMNS), 0, GRAINS), jax.random.fold_in(arg_keys[1], 1), 0, GRAINS - 1).astype(jnp.int32)
    grain_orient = touch_ends(jax.random.randint(arg_keys[2], (GRAINS,), 0, ORIENTS), jax.random.fold_in(arg_keys[2], 1), 0, ORIENTS - 1).astype(jnp.int32)
    orient_mobility = jnp.clip(jnp.exp(jax.random.uniform(arg_keys[3], (ORIENTS,), jnp.float32, math.log(0.4), math.log(1.2))), 0.4, 1.2)
    solute_init = jnp.clip(0.1 + 0.4 * jax.random.uniform(arg_keys[4], (SOLUTES, DEPTH, BREADTH, COLUMNS), jnp.float32) ** steps_of(arg_keys[4], (SOLUTES, DEPTH, BREADTH, COLUMNS), ((1, 64), (2, 8)), -0.2, 0.2), 0.1, 0.5)
    partition = jnp.clip(jax.random.uniform(arg_keys[5], (PHASES, SOLUTES), jnp.float32, -0.5, 0.5), -0.5, 0.5)
    return dict(phase_label=phase_label, grain_label=grain_label, grain_orient=grain_orient, orient_mobility=orient_mobility, solute_init=solute_init, partition=partition)


ANISOTROPY = 1.5
WELL_HEIGHT = 4.0
TIME_STEP = 0.06
LIQUID_DIFFUSION = 1.0
SOLID_DIFFUSION = 0.1
COOLING_WEIGHTS = (-1.0, 0.8, 0.7, 0.6)
FIRST_WEIGHTS = (0.5, -1.0, 0.4, 0.3)
SECOND_WEIGHTS = (0.4, 0.3, -1.0, 0.5)
INFLOW_FIRST = 0.3
INFLOW_SECOND = 0.2
LIQUID_MOBILITY = 1.0


def advance(padded, mobility, undercool, partition):
    centre = padded[:, 1:-1, 1:-1]
    plane_up = padded[:, 2:, 1:-1]
    plane_down = padded[:, :-2, 1:-1]
    row_next = padded[:, 1:-1, 2:]
    row_prev = padded[:, 1:-1, :-2]
    col_next = jnp.roll(centre, -1, axis=3)
    col_prev = jnp.roll(centre, 1, axis=3)
    phases = centre[:4]
    solutes = centre[4:]
    laplace = ANISOTROPY * (plane_up[:4] + plane_down[:4] - 2.0 * phases)
    laplace = laplace + (row_next[:4] + row_prev[:4] - 2.0 * phases)
    laplace = laplace + (col_next[:4] + col_prev[:4] - 2.0 * phases)
    cooling_w = jnp.array(COOLING_WEIGHTS, dtype=phases.dtype).reshape(4, 1, 1, 1)
    first_w = jnp.array(FIRST_WEIGHTS, dtype=phases.dtype).reshape(4, 1, 1, 1)
    second_w = jnp.array(SECOND_WEIGHTS, dtype=phases.dtype).reshape(4, 1, 1, 1)
    driving = cooling_w * undercool[None] + first_w * solutes[0][None] + second_w * solutes[1][None]
    forcing = laplace + WELL_HEIGHT * phases * (1.0 - phases) * (phases - 0.5 + driving)
    growth_rate = mobility[None] * (forcing - jnp.mean(forcing, axis=0, keepdims=True))
    trials = jnp.clip(phases + TIME_STEP * growth_rate, 0.0, 1.0)
    new_phases = trials / jnp.sum(trials, axis=0, keepdims=True)
    own_diffusion = SOLID_DIFFUSION + (LIQUID_DIFFUSION - SOLID_DIFFUSION) * centre[0]
    influx = jnp.zeros_like(solutes)
    for neighbour in (plane_up, plane_down, row_next, row_prev, col_next, col_prev):
        other = SOLID_DIFFUSION + (LIQUID_DIFFUSION - SOLID_DIFFUSION) * neighbour[0]
        influx = influx + 0.5 * (other + own_diffusion)[None] * (neighbour[4:] - solutes)
    changes = new_phases - phases
    rejected = partition[0][:, None, None, None] * changes[0][None]
    rejected = rejected + partition[1][:, None, None, None] * changes[1][None]
    rejected = rejected + partition[2][:, None, None, None] * changes[2][None]
    rejected = rejected + partition[3][:, None, None, None] * changes[3][None]
    new_solutes = solutes + TIME_STEP * influx - rejected
    return jnp.concatenate([new_phases, new_solutes], axis=0)


def pad_grid(fields):
    padded = jnp.concatenate([fields[:, :1], fields, fields[:, -1:]], axis=1)
    return jnp.concatenate([padded[:, :, -1:], padded, padded[:, :, :1]], axis=2)


def cooling(heights, total_depth):
    return (2.0 * (0.5 - (heights + 0.5) / total_depth))[:, None, None]


def reference(phase_label, grain_label, grain_orient, orient_mobility, solute_init, partition):
    grain_mobility = orient_mobility[grain_orient]
    mobility = grain_mobility[grain_label]
    labels = jnp.arange(4, dtype=jnp.int32)[:, None, None, None]
    phases = (phase_label[None] == labels).astype(solute_init.dtype)
    fields = jnp.concatenate([phases, solute_init], axis=0)
    total_depth = fields.shape[1]
    heights = jnp.arange(total_depth, dtype=jnp.int32).astype(fields.dtype)
    undercool = cooling(heights, total_depth)
    fields = advance(pad_grid(fields), mobility, undercool, partition)
    fields = advance(pad_grid(fields), mobility, undercool, partition)
    inflow = jnp.array([1.0, 0.0, 0.0, 0.0, INFLOW_FIRST, INFLOW_SECOND], dtype=fields.dtype)
    liquid = inflow[:, None, None, None] * jnp.ones((6, SHIFT, fields.shape[2], fields.shape[3]), fields.dtype)
    fields = jnp.concatenate([fields[:, SHIFT:], liquid], axis=1)
    liquid_mob = LIQUID_MOBILITY * jnp.ones((SHIFT, fields.shape[2], fields.shape[3]), fields.dtype)
    mobility = jnp.concatenate([mobility[SHIFT:], liquid_mob], axis=0)
    fields = advance(pad_grid(fields), mobility, undercool, partition)
    return fields[:4], fields[4:]
```

```python
import functools

import jax
import jax.numpy as jnp
from jax import lax
from jax.experimental import pallas as pl
from jax.experimental.pallas import tpu as pltpu
from jax.sharding import PartitionSpec as P

MESH = pl.DeviceIdType.MESH
SHIFT = 16
STEPS = 3
ANISOTROPY = 1.5
WELL_HEIGHT = 4.0
TIME_STEP = 0.06
LIQUID_DIFFUSION = 1.0
SOLID_DIFFUSION = 0.1
COOLING_WEIGHTS = (-1.0, 0.8, 0.7, 0.6)
FIRST_WEIGHTS = (0.5, -1.0, 0.4, 0.3)
SECOND_WEIGHTS = (0.4, 0.3, -1.0, 0.5)
INFLOW = (1.0, 0.0, 0.0, 0.0, 0.3, 0.2)
LIQUID_MOBILITY = 1.0
ROWS = 16


def kernel(n_grow, n_trans, parts, ph, gr, so, go, om, pa, pout, sout, PH, GR, CC, S0, MO, T1, T2, loc, send, recv):
    g = lax.axis_index("grow")
    t = lax.axis_index("trans")
    planes, rows, cols = ph.shape
    left = lax.rem(t + n_trans - 1, n_trans)
    right = lax.rem(t + 1, n_trans)
    first, last = g == 0, g == n_grow - 1
    own = planes - SHIFT + STEPS
    skip = planes - own
    more = SHIFT + STEPS
    length = own + more

    barrier = pltpu.get_barrier_semaphore()

    def greet(dg, tt):
        pl.semaphore_signal(barrier, inc=1, device_id={"grow": g + dg, "trans": tt}, device_id_type=MESH)

    greet(0, left)
    greet(0, right)

    @pl.when(jnp.logical_not(last))
    def _():
        greet(1, t)
        greet(1, left)
        greet(1, right)

    local = []
    for n, (src, dst) in enumerate(
        [
            (ph.at[pl.ds(skip, own)], PH.at[pl.ds(0, own), pl.ds(0, rows)]),
            (gr.at[pl.ds(skip, own)], GR.at[pl.ds(0, own), pl.ds(0, rows)]),
            (so.at[:, pl.ds(skip, own)], CC.at[:, pl.ds(0, own), pl.ds(0, rows)]),
        ]
    ):
        copy = pltpu.make_async_copy(src, dst, loc.at[n])
        copy.start()
        local.append(copy)

    count = 0

    def group(src_plane, size, dst_plane, src_row, dst_row, width, dg, tt):
        nonlocal count
        copies = []
        sp, dp = pl.ds(src_plane, size), pl.ds(dst_plane, size)
        sr, dr = pl.ds(src_row, width), pl.ds(dst_row, width)
        for src, dst in (
            (ph.at[sp, sr], PH.at[dp, dr]),
            (gr.at[sp, sr], GR.at[dp, dr]),
            (so.at[:, sp, sr], CC.at[:, dp, dr]),
        ):
            copies.append(
                pltpu.make_async_remote_copy(
                    src_ref=src,
                    dst_ref=dst,
                    send_sem=send.at[count],
                    recv_sem=recv.at[count],
                    device_id={"grow": g + dg, "trans": tt},
                    device_id_type=MESH,
                )
            )
            count += 1
        return copies

    side = group(skip, own, 0, rows - STEPS, ROWS - STEPS, STEPS, 0, right) + group(skip, own, 0, 0, rows, STEPS, 0, left)
    down = group(0, more, own, 0, 0, rows, -1, t)
    down += group(0, more, own, rows - STEPS, ROWS - STEPS, STEPS, -1, right) + group(0, more, own, 0, rows, STEPS, -1, left)

    @pl.when(first)
    def _():
        pl.semaphore_wait(barrier, 2)

    @pl.when(jnp.logical_not(first))
    def _():
        pl.semaphore_wait(barrier, 5)

    for copy in side:
        copy.start()

    @pl.when(jnp.logical_not(first))
    def _():
        for copy in down:
            copy.start()

    lane = lax.broadcasted_iota(jnp.int32, (ROWS, cols), 1)
    table = jnp.zeros((ROWS, cols), jnp.float32)
    for n in range(go.shape[0]):
        table = jnp.where(lane == n, om[go[n]] * TIME_STEP, table)

    for copy in local:
        copy.wait()
    for copy in side:
        copy.wait_recv()

    @pl.when(jnp.logical_not(last))
    def _():
        for copy in down:
            copy.wait_recv()

    def expand(w, _):
        label = PH[w]
        for a in range(4):
            S0[a, w] = jnp.where(label == a, 1.0, 0.0)
        MO[w] = jnp.take_along_axis(table, jnp.bitwise_and(GR[w], go.shape[0] - 1), axis=1)
        return 0

    if "compute" in parts:
        lax.fori_loop(0, length, expand, 0)

    part = [[pa[a, k] for k in range(2)] for a in range(4)]
    spread = (LIQUID_DIFFUSION - SOLID_DIFFUSION) * 0.5 * TIME_STEP
    base = SOLID_DIFFUSION * 0.5 * TIME_STEP

    def advance(load, w, up, down, height, mob, keep):
        total = jnp.float32(n_grow * planes)
        undercool = 2.0 * (0.5 - (height.astype(jnp.float32) + 0.5) / total)

        def roll(v, shift, axis):
            return pltpu.roll(v, shift % v.shape[axis], axis)

        centre = [load(k, w) for k in range(6)]
        above = [load(k, up)[:keep] for k in range(6)]
        below = [load(k, down)[:keep] for k in range(6)]
        rown = [roll(v, -1, 0)[:keep] for v in centre]
        rowp = [roll(v, 1, 0)[:keep] for v in centre]
        centre = [v[:keep] for v in centre]
        coln = [roll(v, -1, 1) for v in centre]
        colp = [roll(v, 1, 1) for v in centre]
        c0, c1 = centre[4], centre[5]
        forcing = []
        for a in range(4):
            p = centre[a]
            lap = ANISOTROPY * (above[a] + below[a]) + ((rown[a] + rowp[a]) + (coln[a] + colp[a])) - (2.0 * ANISOTROPY + 4.0) * p
            drive = (p + (COOLING_WEIGHTS[a] * undercool - 0.5)) + (FIRST_WEIGHTS[a] * c0 + SECOND_WEIGHTS[a] * c1)
            forcing.append(lap + (WELL_HEIGHT * p) * ((1.0 - p) * drive))
        mean = 0.25 * ((forcing[0] + forcing[1]) + (forcing[2] + forcing[3]))
        trials = [jnp.clip(centre[a] + mob * (forcing[a] - mean), 0.0, 1.0) for a in range(4)]
        scale = 1.0 / ((trials[0] + trials[1]) + (trials[2] + trials[3]))
        new = [v * scale for v in trials]
        changes = [new[a] - centre[a] for a in range(4)]
        own_d = base + spread * centre[0]
        sums = [None, None]
        for near in (above, below, rown, rowp, coln, colp):
            d = own_d + (base + spread * near[0])
            for k in range(2):
                flow = d * (near[4 + k] - centre[4 + k])
                sums[k] = flow if sums[k] is None else sums[k] + flow
        for k in range(2):
            rejected = (part[0][k] * changes[0] + part[1][k] * changes[1]) + (part[2][k] * changes[2] + part[3][k] * changes[3])
            new.append(centre[4 + k] + sums[k] - rejected)
        return new

    top = jnp.where(last, own - 1, length - 1)
    origin = g * planes + skip

    def one(w, _):
        new = advance(lambda k, i: S0[k, i] if k < 4 else CC[k - 4, i], w, jnp.minimum(w + 1, top), w - 1, origin + w, MO[w], ROWS)
        for k in range(6):
            T1[k, w] = new[k]
        return 0

    def two(w, _):
        new = advance(lambda k, i: T1[k, i], w, jnp.minimum(w + 1, top), w - 1, origin + w, MO[w], ROWS)
        for k in range(6):
            T2[k, w] = new[k]
        return 0

    bottom = jnp.where(first, STEPS, 0)

    def three(w, _):
        new = advance(lambda k, i: T2[k, i], w, w + 1, jnp.maximum(w - 1, bottom), g * planes + w - STEPS, MO[w][:rows], rows)
        for k in range(4):
            pout[k, w - STEPS] = new[k]
        for k in range(2):
            sout[k, w - STEPS] = new[4 + k]
        return 0

    if "compute" in parts:
        lax.fori_loop(1, length - 1, one, 0)
        lax.fori_loop(2, length - 2, two, 0)

        @pl.when(last)
        def _():
            def fill(w, _):
                for k in range(6):
                    T2[k, w] = jnp.full((ROWS, cols), INFLOW[k], jnp.float32)
                MO[w] = jnp.full((ROWS, cols), LIQUID_MOBILITY * TIME_STEP, jnp.float32)
                return 0

            lax.fori_loop(own, length, fill, 0)

        lax.fori_loop(3, length - 3, three, 0)

    for copy in side:
        copy.wait_send()

    @pl.when(jnp.logical_not(first))
    def _():
        for copy in down:
            copy.wait_send()


def solution(mesh, parts=("compute",)):
    n_grow, n_trans = mesh.shape["grow"], mesh.shape["trans"]

    def shards(phase_label, grain_label, grain_orient, orient_mobility, solute_init, partition):
        planes, rows, cols = phase_label.shape
        length = planes + 2 * STEPS
        window = (length, ROWS, cols)
        hbm = pl.BlockSpec(memory_space=pl.ANY)
        smem = pl.BlockSpec(memory_space=pltpu.SMEM)
        vmem = pl.BlockSpec(memory_space=pltpu.VMEM)
        f32 = jnp.float32
        return pl.pallas_call(
            functools.partial(kernel, n_grow, n_trans, parts),
            out_shape=(
                jax.ShapeDtypeStruct((4, planes, rows, cols), f32),
                jax.ShapeDtypeStruct((2, planes, rows, cols), f32),
            ),
            in_specs=[hbm, hbm, hbm, smem, smem, smem],
            out_specs=(vmem, vmem),
            scratch_shapes=[
                pltpu.VMEM(window, jnp.int32),
                pltpu.VMEM(window, jnp.int32),
                pltpu.VMEM((2, *window), f32),
                pltpu.VMEM((4, *window), f32),
                pltpu.VMEM(window, f32),
                pltpu.VMEM((6, *window), f32),
                pltpu.VMEM((6, *window), f32),
                pltpu.SemaphoreType.DMA((3,)),
                pltpu.SemaphoreType.DMA((15,)),
                pltpu.SemaphoreType.DMA((15,)),
            ],
            compiler_params=pltpu.CompilerParams(collective_id=0, has_side_effects=True),
        )(phase_label, grain_label, solute_init, grain_orient, orient_mobility, partition)

    placed = (P("grow", "trans", None), P("grow", "trans", None), P(), P(), P(None, "grow", "trans", None), P())
    return jax.shard_map(
        shards,
        mesh=mesh,
        in_specs=placed,
        out_specs=(P(None, "grow", "trans", None), P(None, "grow", "trans", None)),
        check_vma=False,
    )
```

```python
import functools

import jax
import jax.numpy as jnp
from jax import lax
from jax.experimental import pallas as pl
from jax.experimental.pallas import tpu as pltpu
from jax.sharding import PartitionSpec as P

MESH = pl.DeviceIdType.MESH
SHIFT = 16
STEPS = 3
ANISOTROPY = 1.5
WELL_HEIGHT = 4.0
TIME_STEP = 0.06
LIQUID_DIFFUSION = 1.0
SOLID_DIFFUSION = 0.1
COOLING_WEIGHTS = (-1.0, 0.8, 0.7, 0.6)
FIRST_WEIGHTS = (0.5, -1.0, 0.4, 0.3)
SECOND_WEIGHTS = (0.4, 0.3, -1.0, 0.5)
INFLOW = (1.0, 0.0, 0.0, 0.0, 0.3, 0.2)
LIQUID_MOBILITY = 1.0
ROWS, OWN, NEXT = 24, 8, 16
UNROLL_WIDE, UNROLL_SLIM = 3, 5
SPLIT = 9


def kernel(n_grow, n_trans, ph, gr, so, go_h, om_h, pa_h, pout, sout, PC, GC, PL, GL, SL, PN, GN, SN, S0, MO, T1, T2, TB, go, om, pa, loc, send, recv, ready):
    g = lax.axis_index("grow")
    t = lax.axis_index("trans")
    planes, rows, cols = ph.shape
    left = lax.rem(t + n_trans - 1, n_trans)
    right = lax.rem(t + 1, n_trans)
    half = n_trans // 2
    place = lax.rem(t, half)
    first, last = g == 0, g == n_grow - 1
    far_right = place == half - 1
    far_left = jnp.logical_not(far_right)
    end = jnp.logical_or(place == 0, far_right)
    early = jnp.logical_and(end, t < half)
    own = planes - SHIFT + STEPS
    skip = planes - own
    more = SHIFT + STEPS
    length = own + more

    barrier = pltpu.get_barrier_semaphore()

    def greet(dg, tt):
        pl.semaphore_signal(barrier, inc=1, device_id={"grow": g + dg, "trans": tt}, device_id_type=MESH)

    greet(0, left)
    greet(0, right)

    @pl.when(jnp.logical_not(last))
    def _():
        greet(1, left)
        greet(1, right)
        greet(1, t)

    local = [
        pltpu.make_async_copy(src, dst, loc.at[n])
        for n, (src, dst) in enumerate(
            [
                (ph.at[pl.ds(skip, own)], PC.at[pl.ds(0, own)]),
                (gr.at[pl.ds(skip, own)], GC.at[pl.ds(0, own)]),
                (so.at[:, pl.ds(skip, own)], S0.at[pl.ds(4, 2), pl.ds(0, own), pl.ds(OWN, rows)]),
                (go_h, go),
                (om_h, om),
                (pa_h, pa),
            ]
        )
    ]
    for copy in local:
        copy.start()

    count = 0

    def group(pairs, dg, tt):
        nonlocal count
        copies = []
        for src, dst in pairs:
            copies.append(
                pltpu.make_async_remote_copy(
                    src_ref=src,
                    dst_ref=dst,
                    send_sem=send.at[count],
                    recv_sem=recv.at[count],
                    device_id={"grow": g + dg, "trans": tt},
                    device_id_type=MESH,
                )
            )
            count += 1
        return copies

    def halo(labels, grains, solutes, wide, slim, tt):
        pieces = []
        for src, size, dst, dg in (
            (skip + 1, own - 1, 1, 0),
            (0, SPLIT, own, -1),
            (SPLIT, more - 1 - SPLIT, own + SPLIT, -1),
        ):
            sp, dp = pl.ds(src, size), pl.ds(dst, size)
            pairs = (
                (ph.at[sp, wide], labels.at[dp, wide]),
                (so.at[:, sp, wide], solutes.at[:, dp, wide]),
                (gr.at[sp, slim], grains.at[dp, slim]),
            )
            pieces.append(group(pairs, dg, tt))
        return pieces

    sp, dp = pl.ds(0, more), pl.ds(own, more)
    main = group(
        (
            (ph.at[sp], PC.at[dp]),
            (so.at[:, sp], S0.at[pl.ds(4, 2), dp, pl.ds(OWN, rows)]),
            (gr.at[sp], GC.at[dp]),
        ),
        -1,
        t,
    )
    to_left = halo(PN, GN, SN, pl.ds(0, STEPS), pl.ds(0, STEPS - 1), left)
    to_right = halo(PL, GL, SL, pl.ds(rows - STEPS, STEPS), pl.ds(rows - STEPS + 1, STEPS - 1), right)

    inner = jnp.logical_not(first)
    outer = jnp.logical_not(last)

    def start_halo(copies):
        for copy in copies[0]:
            copy.start()

        @pl.when(inner)
        def _():
            for copy in copies[1] + copies[2]:
                copy.start()

    def start_far():
        @pl.when(far_left)
        def _():
            start_halo(to_left)

        @pl.when(far_right)
        def _():
            start_halo(to_right)

    def start_near():
        @pl.when(far_left)
        def _():
            start_halo(to_right)

        @pl.when(far_right)
        def _():
            start_halo(to_left)

        @pl.when(inner)
        def _():
            for copy in main:
                copy.start()

    def meet():
        @pl.when(first)
        def _():
            pl.semaphore_wait(barrier, 2)

        @pl.when(inner)
        def _():
            pl.semaphore_wait(barrier, 5)

    @pl.when(jnp.logical_not(early))
    def _():
        meet()

        @pl.when(place == 1)
        def _():
            pl.semaphore_signal(ready, inc=1, device_id={"grow": g, "trans": left}, device_id_type=MESH)

        @pl.when(place == half - 2)
        def _():
            pl.semaphore_signal(ready, inc=1, device_id={"grow": g, "trans": right}, device_id_type=MESH)

        start_far()

    @pl.when(end)
    def _():
        pl.semaphore_wait(ready, 1)

    start_near()

    for copy in local[3:]:
        copy.wait()
    lane = lax.broadcasted_iota(jnp.int32, (rows, cols), 1)
    table = jnp.zeros((rows, cols), jnp.float32)
    for n in range(go.shape[0]):
        table = jnp.where(lane == n, om[go[n]] * TIME_STEP, table)
    TB[...] = table

    def expand(low, high, row, labels, grains, solutes):
        def body(w, _):
            at = pl.ds(row, rows)
            label = labels[w]
            for a in range(4):
                S0[a, w, at] = jnp.where(label == a, 1.0, 0.0)
            if solutes is not None:
                for k in range(2):
                    S0[4 + k, w, at] = solutes[k, w]
            grain = jnp.bitwise_and(grains[w], go.shape[0] - 1)
            mob = jnp.take_along_axis(TB[...], grain, axis=1)
            MO[w, at] = jnp.where(jnp.logical_and(last, w >= own), LIQUID_MOBILITY * TIME_STEP, mob)
            return 0

        lax.fori_loop(low, high, body, 0, unroll=2)

    part = [[pa[k, a] for k in range(2)] for a in range(4)]
    spread = (LIQUID_DIFFUSION - SOLID_DIFFUSION) * 0.5 * TIME_STEP
    base = SOLID_DIFFUSION * 0.5 * TIME_STEP

    def roll(v, shift):
        return pltpu.roll(v, shift % v.shape[1], 1)

    def advance(load, w, up, down, height, mob):
        total = jnp.float32(n_grow * planes)
        undercool = 2.0 * (0.5 - (height.astype(jnp.float32) + 0.5) / total)
        centre = [load(k, w, 0) for k in range(6)]
        above = [load(k, up, 0) for k in range(6)]
        below = [load(k, down, 0) for k in range(6)]
        rown = [load(k, w, 1) for k in range(6)]
        rowp = [load(k, w, -1) for k in range(6)]
        coln = [roll(v, -1) for v in centre]
        colp = [roll(v, 1) for v in centre[:4]]
        c0, c1 = centre[4], centre[5]
        forcing = []
        for a in range(4):
            p = centre[a]
            lap = ANISOTROPY * (above[a] + below[a]) + ((rown[a] + rowp[a]) + (coln[a] + colp[a])) - (2.0 * ANISOTROPY + 4.0) * p
            drive = (p + (COOLING_WEIGHTS[a] * undercool - 0.5)) + (FIRST_WEIGHTS[a] * c0 + SECOND_WEIGHTS[a] * c1)
            forcing.append(lap + (WELL_HEIGHT * p) * ((1.0 - p) * drive))
        mean = 0.25 * ((forcing[0] + forcing[1]) + (forcing[2] + forcing[3]))
        trials = [jnp.clip(centre[a] + mob * (forcing[a] - mean), 0.0, 1.0) for a in range(4)]
        scale = 1.0 / ((trials[0] + trials[1]) + (trials[2] + trials[3]))
        new = [v * scale for v in trials]
        changes = [new[a] - centre[a] for a in range(4)]
        own_d = 2.0 * base + spread * centre[0]
        sums = [None, None]
        d = own_d + spread * coln[0]
        for k in range(2):
            flow = d * (coln[4 + k] - centre[4 + k])
            sums[k] = flow - roll(flow, 1)
        for near in (above, below, rown, rowp):
            d = own_d + spread * near[0]
            for k in range(2):
                sums[k] = sums[k] + d * (near[4 + k] - centre[4 + k])
        for k in range(2):
            rejected = (part[0][k] * changes[0] + part[1][k] * changes[1]) + (part[2][k] * changes[2] + part[3][k] * changes[3])
            new.append((centre[4 + k] + sums[k]) - rejected)
        return new

    top = jnp.where(last, own - 1, length - 1)
    origin = g * planes + skip

    def one(low, high, row, size, unroll):
        def load(k, i, by):
            at = pl.ds(row + by, size)
            return S0[k, i, at]

        def body(w, _):
            new = advance(load, w, jnp.minimum(w + 1, top), w - 1, origin + w, MO[w, pl.ds(row, size)])
            for k in range(6):
                T1[k, w, pl.ds(row, size)] = new[k]
            return 0

        lax.fori_loop(low, high, body, 0, unroll=unroll)

    def two(low, high, row, size, unroll):
        def load(k, i, by):
            return T1[k, i, pl.ds(row + by, size)]

        def body(w, _):
            new = advance(load, w, jnp.minimum(w + 1, top), w - 1, origin + w, MO[w, pl.ds(row, size)])
            for k in range(6):
                T2[k, w, pl.ds(row, size)] = new[k]
            return 0

        lax.fori_loop(low, high, body, 0, unroll=unroll)

    bottom = jnp.where(first, STEPS, 0)

    def three(low, high, unroll):
        def load(k, i, by):
            return T2[k, i, pl.ds(OWN + by, rows)]

        def body(w, _):
            new = advance(load, w, w + 1, jnp.maximum(w - 1, bottom), g * planes + w - STEPS, MO[w, pl.ds(OWN, rows)])
            for k in range(4):
                pout[k, w - STEPS] = new[k]
            for k in range(2):
                sout[k, w - STEPS] = new[4 + k]
            return 0

        lax.fori_loop(low, high, body, 0, unroll=unroll)

    def flood(low, high):
        @pl.when(last)
        def _():
            def body(w, _):
                for k in range(6):
                    T2[k, w] = jnp.full((ROWS, cols), INFLOW[k], jnp.float32)
                return 0

            lax.fori_loop(max(low, own), high, body, 0)

    def arrive(copies):
        for copy in copies:
            copy.wait_recv()

    def take(pieces, before, near):
        low = (1, own, own + SPLIT)[pieces[0]]
        high = (own, own + SPLIT, length - 1)[pieces[-1]]

        def side(copies, row, buffers):
            def wait():
                for n in pieces:
                    arrive(copies[n])

            if pieces[0] == 0:
                wait()
            else:
                pl.when(outer)(wait)
            expand(low, high, row, *buffers)

        @pl.when(jnp.logical_and(before, far_left if near else far_right))
        def _():
            side(to_left, NEXT, (PN, GN, SN))

        @pl.when(jnp.logical_and(before, far_right if near else far_left))
        def _():
            side(to_right, 0, (PL, GL, SL))

    middle = jnp.logical_not(end)
    always = g >= 0
    wide = 2 * rows
    for copy in local[:3]:
        copy.wait()
    expand(0, own, OWN, PC, GC, None)
    take([0], always, True)
    take([0], middle, False)
    one(1, own - 1, OWN - 2, wide, UNROLL_WIDE)
    two(2, own - 2, OWN - 2, wide, UNROLL_WIDE)

    @pl.when(early)
    def _():
        meet()
        start_far()

    @pl.when(outer)
    def _():
        arrive(main)

    expand(own, length, OWN, PC, GC, None)
    take([1, 2], always, True)
    take([1, 2], middle, False)
    one(own - 1, length - 1, OWN - 2, wide, UNROLL_WIDE)
    two(own - 2, length - 2, OWN - 2, wide, UNROLL_WIDE)

    near = jnp.where(far_right, NEXT + 2 - rows, OWN - 2)
    bounds = (1, own, own + SPLIT, length)
    for n in range(3):
        high = bounds[n + 1]
        lows = [max(bounds[n] - s, s) for s in (1, 2, 3)]
        take([n], end, False)

        @pl.when(end)
        def _():
            one(lows[0], high - 1, near, rows, UNROLL_SLIM)
            two(lows[1], high - 2, near, rows, UNROLL_SLIM)

        if high - 2 > own:
            flood(lows[1], high - 2)
        three(lows[2], high - 3, UNROLL_SLIM)

    for copy in to_left[0] + to_right[0]:
        copy.wait_send()

    @pl.when(inner)
    def _():
        for copy in main + to_left[1] + to_left[2] + to_right[1] + to_right[2]:
            copy.wait_send()


def solution(mesh):
    n_grow, n_trans = mesh.shape["grow"], mesh.shape["trans"]

    def shards(phase_label, grain_label, grain_orient, orient_mobility, solute_init, partition):
        planes, rows, cols = phase_label.shape
        length = planes + 2 * STEPS
        window = (length, ROWS, cols)
        block = (length, rows, cols)
        hbm = pl.BlockSpec(memory_space=pl.ANY)
        vmem = pl.BlockSpec(memory_space=pltpu.VMEM)
        f32, i32 = jnp.float32, jnp.int32
        return pl.pallas_call(
            functools.partial(kernel, n_grow, n_trans),
            out_shape=(
                pltpu.VMEM((4, planes, rows, cols), f32),
                pltpu.VMEM((2, planes, rows, cols), f32),
            ),
            in_specs=[hbm] * 6,
            out_specs=(vmem, vmem),
            scratch_shapes=[
                pltpu.VMEM(block, i32),
                pltpu.VMEM(block, i32),
                pltpu.VMEM(block, i32),
                pltpu.VMEM(block, i32),
                pltpu.VMEM((2, *block), f32),
                pltpu.VMEM(block, i32),
                pltpu.VMEM(block, i32),
                pltpu.VMEM((2, *block), f32),
                pltpu.VMEM((6, *window), f32),
                pltpu.VMEM(window, f32),
                pltpu.VMEM((6, *window), f32),
                pltpu.VMEM((6, *window), f32),
                pltpu.VMEM((rows, cols), f32),
                pltpu.SMEM(grain_orient.shape, i32),
                pltpu.SMEM(orient_mobility.shape, f32),
                pltpu.SMEM(partition.shape[::-1], f32),
                pltpu.SemaphoreType.DMA((6,)),
                pltpu.SemaphoreType.DMA((21,)),
                pltpu.SemaphoreType.DMA((21,)),
                pltpu.SemaphoreType.REGULAR,
            ],
            compiler_params=pltpu.CompilerParams(collective_id=0, has_side_effects=True),
        )(phase_label, grain_label, solute_init, grain_orient, orient_mobility, partition.T)

    placed = (P("grow", "trans", None), P("grow", "trans", None), P(), P(), P(None, "grow", "trans", None), P())
    return jax.shard_map(
        shards,
        mesh=mesh,
        in_specs=placed,
        out_specs=(P(None, "grow", "trans", None), P(None, "grow", "trans", None)),
        check_vma=False,
    )
```

```python
import functools

import jax
import jax.numpy as jnp
from jax import lax
from jax.experimental import pallas as pl
from jax.experimental.pallas import tpu as pltpu
from jax.sharding import PartitionSpec as P

MESH = pl.DeviceIdType.MESH
SHIFT = 16
STEPS = 3
ANISOTROPY = 1.5
WELL_HEIGHT = 4.0
TIME_STEP = 0.06
LIQUID_DIFFUSION = 1.0
SOLID_DIFFUSION = 0.1
COOLING_WEIGHTS = (-1.0, 0.8, 0.7, 0.6)
FIRST_WEIGHTS = (0.5, -1.0, 0.4, 0.3)
SECOND_WEIGHTS = (0.4, 0.3, -1.0, 0.5)
INFLOW = (1.0, 0.0, 0.0, 0.0, 0.3, 0.2)
LIQUID_MOBILITY = 1.0
ROWS, OWN, NEXT = 24, 8, 16
UNROLL_WIDE, UNROLL_SLIM = 3, 5
TURN = 8
SPLIT = 9


def kernel(n_grow, n_trans, ph, gr, so, go_h, om_h, pa_h, pout, sout, PC, GC, PL, GL, SL, PN, GN, SN, S0, MO, T1, T2, TB, go, om, pa, loc, send, recv, ready):
    g = lax.axis_index("grow")
    t = lax.axis_index("trans")
    planes, rows, cols = ph.shape
    left = lax.rem(t + n_trans - 1, n_trans)
    right = lax.rem(t + 1, n_trans)
    half = n_trans // 2
    place = lax.rem(t, half)
    first, last = g == 0, g == n_grow - 1
    far_right = place == half - 1
    far_left = jnp.logical_not(far_right)
    end = jnp.logical_or(place == 0, far_right)
    early = jnp.logical_and(end, t < half)
    sooner = jnp.logical_and(early, lax.rem(g, TURN) == 0)
    later = jnp.logical_and(early, lax.rem(g, TURN) != 0)
    own = planes - SHIFT + STEPS
    skip = planes - own
    more = SHIFT + STEPS
    length = own + more

    barrier = pltpu.get_barrier_semaphore()

    def greet(dg, tt):
        pl.semaphore_signal(barrier, inc=1, device_id={"grow": g + dg, "trans": tt}, device_id_type=MESH)

    greet(0, left)
    greet(0, right)

    @pl.when(jnp.logical_not(last))
    def _():
        greet(1, left)
        greet(1, right)
        greet(1, t)

    local = [
        pltpu.make_async_copy(src, dst, loc.at[n])
        for n, (src, dst) in enumerate(
            [
                (ph.at[pl.ds(skip, own)], PC.at[pl.ds(0, own)]),
                (gr.at[pl.ds(skip, own)], GC.at[pl.ds(0, own)]),
                (so.at[:, pl.ds(skip, own)], S0.at[pl.ds(4, 2), pl.ds(0, own), pl.ds(OWN, rows)]),
                (go_h, go),
                (om_h, om),
                (pa_h, pa),
            ]
        )
    ]
    for copy in local:
        copy.start()

    count = 0

    def group(pairs, dg, tt):
        nonlocal count
        copies = []
        for src, dst in pairs:
            copies.append(
                pltpu.make_async_remote_copy(
                    src_ref=src,
                    dst_ref=dst,
                    send_sem=send.at[count],
                    recv_sem=recv.at[count],
                    device_id={"grow": g + dg, "trans": tt},
                    device_id_type=MESH,
                )
            )
            count += 1
        return copies

    def halo(labels, grains, solutes, wide, slim, tt):
        pieces = []
        for src, size, dst, dg in (
            (skip + 1, own - 1, 1, 0),
            (0, SPLIT, own, -1),
            (SPLIT, more - 1 - SPLIT, own + SPLIT, -1),
        ):
            sp, dp = pl.ds(src, size), pl.ds(dst, size)
            pairs = (
                (ph.at[sp, wide], labels.at[dp, wide]),
                (so.at[:, sp, wide], solutes.at[:, dp, wide]),
                (gr.at[sp, slim], grains.at[dp, slim]),
            )
            pieces.append(group(pairs, dg, tt))
        return pieces

    main = [None]
    for src, size in ((0, SPLIT), (SPLIT, more - SPLIT)):
        sp, dp = pl.ds(src, size), pl.ds(own + src, size)
        pairs = (
            (ph.at[sp], PC.at[dp]),
            (so.at[:, sp], S0.at[pl.ds(4, 2), dp, pl.ds(OWN, rows)]),
            (gr.at[sp], GC.at[dp]),
        )
        main.append(group(pairs, -1, t))
    to_left = halo(PN, GN, SN, pl.ds(0, STEPS), pl.ds(0, STEPS - 1), left)
    to_right = halo(PL, GL, SL, pl.ds(rows - STEPS, STEPS), pl.ds(rows - STEPS + 1, STEPS - 1), right)

    inner = jnp.logical_not(first)
    outer = jnp.logical_not(last)

    def start_halo(copies):
        for copy in copies[0]:
            copy.start()

        @pl.when(inner)
        def _():
            for copy in copies[1] + copies[2]:
                copy.start()

    def start_far():
        @pl.when(far_left)
        def _():
            start_halo(to_left)

        @pl.when(far_right)
        def _():
            start_halo(to_right)

    def start_main():
        @pl.when(inner)
        def _():
            for copy in main[1] + main[2]:
                copy.start()

    def start_near():
        @pl.when(far_left)
        def _():
            start_halo(to_right)

        @pl.when(far_right)
        def _():
            start_halo(to_left)

        start_main()

    def meet():
        @pl.when(first)
        def _():
            pl.semaphore_wait(barrier, 2)

        @pl.when(inner)
        def _():
            pl.semaphore_wait(barrier, 5)

    @pl.when(jnp.logical_not(early))
    def _():
        meet()

        @pl.when(place == 1)
        def _():
            pl.semaphore_signal(ready, inc=1, device_id={"grow": g, "trans": left}, device_id_type=MESH)

        @pl.when(place == half - 2)
        def _():
            pl.semaphore_signal(ready, inc=1, device_id={"grow": g, "trans": right}, device_id_type=MESH)

        start_far()

    @pl.when(end)
    def _():
        pl.semaphore_wait(ready, 1)

    start_near()

    for copy in local[3:]:
        copy.wait()
    lane = lax.broadcasted_iota(jnp.int32, (rows, cols), 1)
    table = jnp.zeros((rows, cols), jnp.float32)
    for n in range(go.shape[0]):
        table = jnp.where(lane == n, om[go[n]] * TIME_STEP, table)
    TB[...] = table

    def expand(low, high, row, labels, grains, solutes):
        def body(w, _):
            at = pl.ds(row, rows)
            label = labels[w]
            for a in range(4):
                S0[a, w, at] = jnp.where(label == a, 1.0, 0.0)
            if solutes is not None:
                for k in range(2):
                    S0[4 + k, w, at] = solutes[k, w]
            grain = jnp.bitwise_and(grains[w], go.shape[0] - 1)
            mob = jnp.take_along_axis(TB[...], grain, axis=1)
            MO[w, at] = jnp.where(jnp.logical_and(last, w >= own), LIQUID_MOBILITY * TIME_STEP, mob)
            return 0

        lax.fori_loop(low, high, body, 0, unroll=2)

    part = [[pa[k, a] for k in range(2)] for a in range(4)]
    spread = (LIQUID_DIFFUSION - SOLID_DIFFUSION) * 0.5 * TIME_STEP
    base = SOLID_DIFFUSION * 0.5 * TIME_STEP

    def roll(v, shift):
        return pltpu.roll(v, shift % v.shape[1], 1)

    def cooling(height):
        return 2.0 * (0.5 - (height.astype(jnp.float32) + 0.5) / jnp.float32(n_grow * planes))

    def advance(load, w, up, down, undercool, mob):
        centre = [load(k, w, 0) for k in range(6)]
        above = [load(k, up, 0) for k in range(6)]
        below = [load(k, down, 0) for k in range(6)]
        rown = [load(k, w, 1) for k in range(6)]
        rowp = [load(k, w, -1) for k in range(6)]
        coln = [roll(v, -1) for v in centre]
        colp = [roll(v, 1) for v in centre[:4]]
        c0, c1 = centre[4], centre[5]
        forcing = []
        for a in range(4):
            p = centre[a]
            lap = ANISOTROPY * (above[a] + below[a]) + ((rown[a] + rowp[a]) + (coln[a] + colp[a])) - (2.0 * ANISOTROPY + 4.0) * p
            drive = (p + (COOLING_WEIGHTS[a] * undercool - 0.5)) + (FIRST_WEIGHTS[a] * c0 + SECOND_WEIGHTS[a] * c1)
            forcing.append(lap + (WELL_HEIGHT * p) * ((1.0 - p) * drive))
        mean = 0.25 * ((forcing[0] + forcing[1]) + (forcing[2] + forcing[3]))
        trials = [jnp.clip(centre[a] + mob * (forcing[a] - mean), 0.0, 1.0) for a in range(4)]
        scale = 1.0 / ((trials[0] + trials[1]) + (trials[2] + trials[3]))
        new = [v * scale for v in trials]
        changes = [new[a] - centre[a] for a in range(4)]
        own_d = 2.0 * base + spread * centre[0]
        sums = [None, None]
        d = own_d + spread * coln[0]
        for k in range(2):
            flow = d * (coln[4 + k] - centre[4 + k])
            sums[k] = flow - roll(flow, 1)
        for near in (above, below, rown, rowp):
            d = own_d + spread * near[0]
            for k in range(2):
                sums[k] = sums[k] + d * (near[4 + k] - centre[4 + k])
        for k in range(2):
            rejected = (part[0][k] * changes[0] + part[1][k] * changes[1]) + (part[2][k] * changes[2] + part[3][k] * changes[3])
            new.append((centre[4 + k] + sums[k]) - rejected)
        return new

    top = jnp.where(last, own - 1, length - 1)
    origin = g * planes + skip

    def one(low, high, row, size, unroll):
        def load(k, i, by):
            at = pl.ds(row + by, size)
            return S0[k, i, at]

        def body(w, _):
            new = advance(load, w, jnp.minimum(w + 1, top), w - 1, cooling(origin + w), MO[w, pl.ds(row, size)])
            for k in range(6):
                T1[k, w, pl.ds(row, size)] = new[k]
            return 0

        lax.fori_loop(low, high, body, 0, unroll=unroll)

    def two(low, high, row, size, unroll):
        def load(k, i, by):
            return T1[k, i, pl.ds(row + by, size)]

        def body(w, _):
            new = advance(load, w, jnp.minimum(w + 1, top), w - 1, cooling(origin + w), MO[w, pl.ds(row, size)])
            for k in range(6):
                T2[k, w, pl.ds(row, size)] = new[k]
            return 0

        lax.fori_loop(low, high, body, 0, unroll=unroll)

    bottom = jnp.where(first, STEPS, 0)

    def three(low, high, unroll):
        def load(k, i, by):
            return T2[k, i, pl.ds(OWN + by, rows)]

        def body(w, _):
            new = advance(load, w, w + 1, jnp.maximum(w - 1, bottom), cooling(g * planes + w - STEPS), MO[w, pl.ds(OWN, rows)])
            for k in range(4):
                pout[k, w - STEPS] = new[k]
            for k in range(2):
                sout[k, w - STEPS] = new[4 + k]
            return 0

        lax.fori_loop(low, high, body, 0, unroll=unroll)

    def flood(low, high):
        @pl.when(last)
        def _():
            def body(w, _):
                for k in range(6):
                    T2[k, w] = jnp.full((ROWS, cols), INFLOW[k], jnp.float32)
                return 0

            lax.fori_loop(max(low, own), high, body, 0)

    def arrive(copies):
        for copy in copies:
            copy.wait_recv()

    def take(pieces, before, near):
        low = (1, own, own + SPLIT)[pieces[0]]
        high = (own, own + SPLIT, length - 1)[pieces[-1]]

        def side(copies, row, buffers):
            def wait():
                for n in pieces:
                    arrive(copies[n])

            if pieces[0] == 0:
                wait()
            else:
                pl.when(outer)(wait)
            expand(low, high, row, *buffers)

        @pl.when(jnp.logical_and(before, far_left if near else far_right))
        def _():
            side(to_left, NEXT, (PN, GN, SN))

        @pl.when(jnp.logical_and(before, far_right if near else far_left))
        def _():
            side(to_right, 0, (PL, GL, SL))

    middle = jnp.logical_not(end)
    always = g >= 0
    wide = 2 * rows
    for copy in local[:3]:
        copy.wait()
    expand(0, own, OWN, PC, GC, None)

    @pl.when(sooner)
    def _():
        meet()
        start_far()

    take([0], always, True)
    take([0], middle, False)
    one(1, own - 1, OWN - 2, wide, UNROLL_WIDE)
    two(2, own - 2, OWN - 2, wide, UNROLL_WIDE)

    @pl.when(later)
    def _():
        meet()
        start_far()

    bounds = (1, own, own + SPLIT, length)

    def lows(n):
        return [max(bounds[n] - s, s) for s in (1, 2, 3)]

    def shut(n):
        if bounds[n + 1] - 2 > own:
            flood(lows(n)[1], bounds[n + 1] - 2)

    def finish(n):
        shut(n)
        three(lows(n)[2], bounds[n + 1] - 3, UNROLL_SLIM)

    finish(0)

    for n in (1, 2):

        @pl.when(outer)
        def _():
            arrive(main[n])

        expand(bounds[n], bounds[n + 1], OWN, PC, GC, None)
        take([n], always, True)
        take([n], middle, False)
        one(lows(n)[0], bounds[n + 1] - 1, OWN - 2, wide, UNROLL_WIDE)
        two(lows(n)[1], bounds[n + 1] - 2, OWN - 2, wide, UNROLL_WIDE)
        finish(n)

    quad = rows // 2
    upper = lax.broadcasted_iota(jnp.int32, (rows, cols), 0) < quad

    def pairs(low, high, source, row, above, below, height, store):
        def load(k, planes_of, by):
            ref = MO if k is None else source.at[k]
            return jnp.where(upper, ref[planes_of[0], pl.ds(row + by, rows)], ref[planes_of[1], pl.ds(row + by - quad, rows)])

        def body(n, _):
            w = low + 2 * n
            undercool = jnp.where(upper, cooling(height + w), cooling(height + w + 1))
            here = (w, w + 1)
            new = advance(load, here, (above(w), above(w + 1)), (below(w), below(w + 1)), undercool, load(None, here, 0))
            for k in range(6):
                store(k, w, new[k][:quad])
                store(k, w + 1, new[k][quad:])
            return 0

        count = (high - low + 1) // 2
        lax.fori_loop(0, count, body, 0, unroll=count)

    def keep(ref, row):
        def store(k, w, value):
            ref[k, w, pl.ds(row, quad)] = value

        return store

    def emit(k, w, value):
        at = pl.ds(jnp.where(far_right, quad, 0), quad)
        if k < 4:
            pout[k, w - STEPS, at] = value
        else:
            sout[k - 4, w - STEPS, at] = value

    rows_of = [jnp.where(far_right, NEXT + 2 - quad - s, OWN - 2 + s) for s in range(3)]

    def capped(w):
        return jnp.minimum(w + 1, top)

    for n in range(3):
        take([n], end, False)

        @pl.when(end)
        def _():
            low, high = lows(n), bounds[n + 1]
            pairs(low[0], high - 1, S0, rows_of[0], capped, lambda w: w - 1, origin, keep(T1, rows_of[0]))
            pairs(low[1], high - 2, T1, rows_of[1], capped, lambda w: w - 1, origin, keep(T2, rows_of[1]))
            shut(n)
            pairs(low[2], high - 3, T2, rows_of[2], lambda w: w + 1, lambda w: jnp.maximum(w - 1, bottom), g * planes - STEPS, emit)

    for copy in to_left[0] + to_right[0]:
        copy.wait_send()

    @pl.when(inner)
    def _():
        for copy in main[1] + main[2] + to_left[1] + to_left[2] + to_right[1] + to_right[2]:
            copy.wait_send()


def solution(mesh):
    n_grow, n_trans = mesh.shape["grow"], mesh.shape["trans"]

    def shards(phase_label, grain_label, grain_orient, orient_mobility, solute_init, partition):
        planes, rows, cols = phase_label.shape
        length = planes + 2 * STEPS
        window = (length, ROWS, cols)
        block = (length, rows, cols)
        hbm = pl.BlockSpec(memory_space=pl.ANY)
        vmem = pl.BlockSpec(memory_space=pltpu.VMEM)
        f32, i32 = jnp.float32, jnp.int32
        return pl.pallas_call(
            functools.partial(kernel, n_grow, n_trans),
            out_shape=(
                pltpu.VMEM((4, planes, rows, cols), f32),
                pltpu.VMEM((2, planes, rows, cols), f32),
            ),
            in_specs=[hbm] * 6,
            out_specs=(vmem, vmem),
            scratch_shapes=[
                pltpu.VMEM(block, i32),
                pltpu.VMEM(block, i32),
                pltpu.VMEM(block, i32),
                pltpu.VMEM(block, i32),
                pltpu.VMEM((2, *block), f32),
                pltpu.VMEM(block, i32),
                pltpu.VMEM(block, i32),
                pltpu.VMEM((2, *block), f32),
                pltpu.VMEM((6, *window), f32),
                pltpu.VMEM(window, f32),
                pltpu.VMEM((6, *window), f32),
                pltpu.VMEM((6, *window), f32),
                pltpu.VMEM((rows, cols), f32),
                pltpu.SMEM(grain_orient.shape, i32),
                pltpu.SMEM(orient_mobility.shape, f32),
                pltpu.SMEM(partition.shape[::-1], f32),
                pltpu.SemaphoreType.DMA((6,)),
                pltpu.SemaphoreType.DMA((24,)),
                pltpu.SemaphoreType.DMA((24,)),
                pltpu.SemaphoreType.REGULAR,
            ],
            compiler_params=pltpu.CompilerParams(collective_id=0, has_side_effects=True),
        )(phase_label, grain_label, solute_init, grain_orient, orient_mobility, partition.T)

    placed = (P("grow", "trans", None), P("grow", "trans", None), P(), P(), P(None, "grow", "trans", None), P())
    return jax.shard_map(
        shards,
        mesh=mesh,
        in_specs=placed,
        out_specs=(P(None, "grow", "trans", None), P(None, "grow", "trans", None)),
        check_vma=False,
    )
```

```python
import functools

import jax
import jax.numpy as jnp
from jax import lax
from jax.experimental import pallas as pl
from jax.experimental.pallas import tpu as pltpu
from jax.sharding import PartitionSpec as P

MESH = pl.DeviceIdType.MESH
SHIFT = 16
STEPS = 3
ANISOTROPY = 1.5
WELL_HEIGHT = 4.0
TIME_STEP = 0.06
LIQUID_DIFFUSION = 1.0
SOLID_DIFFUSION = 0.1
COOLING_WEIGHTS = (-1.0, 0.8, 0.7, 0.6)
FIRST_WEIGHTS = (0.5, -1.0, 0.4, 0.3)
SECOND_WEIGHTS = (0.4, 0.3, -1.0, 0.5)
INFLOW = (1.0, 0.0, 0.0, 0.0, 0.3, 0.2)
LIQUID_MOBILITY = 1.0
ROWS, OWN, NEXT = 24, 8, 16
UNROLL_WIDE, UNROLL_SLIM = 3, 5
PARTS = 6
TURN = 8
SPLIT = 9


def kernel(n_grow, n_trans, ph, gr, so, go_h, om_h, pa_h, pout, sout, PC, GC, PL, GL, SL, PN, GN, SN, S0, MO, T1, T2, TB, go, om, pa, loc, send, recv, ready):
    g = lax.axis_index("grow")
    t = lax.axis_index("trans")
    planes, rows, cols = ph.shape
    left = lax.rem(t + n_trans - 1, n_trans)
    right = lax.rem(t + 1, n_trans)
    half = n_trans // 2
    place = lax.rem(t, half)
    first, last = g == 0, g == n_grow - 1
    far_right = place == half - 1
    far_left = jnp.logical_not(far_right)
    end = jnp.logical_or(place == 0, far_right)
    early = jnp.logical_and(end, t < half)
    sooner = jnp.logical_and(early, lax.rem(g, TURN) == 0)
    later = jnp.logical_and(early, lax.rem(g, TURN) != 0)
    own = planes - SHIFT + STEPS
    skip = planes - own
    more = SHIFT + STEPS
    length = own + more

    barrier = pltpu.get_barrier_semaphore()

    def greet(dg, tt):
        pl.semaphore_signal(barrier, inc=1, device_id={"grow": g + dg, "trans": tt}, device_id_type=MESH)

    greet(0, left)
    greet(0, right)

    @pl.when(jnp.logical_not(last))
    def _():
        greet(1, left)
        greet(1, right)
        greet(1, t)

    local = [
        pltpu.make_async_copy(src, dst, loc.at[n])
        for n, (src, dst) in enumerate(
            [
                (ph.at[pl.ds(skip, own)], PC.at[pl.ds(0, own)]),
                (gr.at[pl.ds(skip, own)], GC.at[pl.ds(0, own)]),
                (so.at[:, pl.ds(skip, own)], S0.at[pl.ds(4, 2), pl.ds(0, own), pl.ds(OWN, rows)]),
                (go_h, go),
                (om_h, om),
                (pa_h, pa),
            ]
        )
    ]
    for copy in local:
        copy.start()

    count = 0

    def group(pairs, dg, tt):
        nonlocal count
        copies = []
        for src, dst in pairs:
            copies.append(
                pltpu.make_async_remote_copy(
                    src_ref=src,
                    dst_ref=dst,
                    send_sem=send.at[count],
                    recv_sem=recv.at[count],
                    device_id={"grow": g + dg, "trans": tt},
                    device_id_type=MESH,
                )
            )
            count += 1
        return copies

    def halo(labels, grains, solutes, wide, slim, tt):
        pieces = []
        for src, size, dst, dg in (
            (skip + 1, own - 1, 1, 0),
            (0, SPLIT, own, -1),
            (SPLIT, more - 1 - SPLIT, own + SPLIT, -1),
        ):
            sp, dp = pl.ds(src, size), pl.ds(dst, size)
            pairs = (
                (ph.at[sp, wide], labels.at[dp, wide]),
                (so.at[:, sp, wide], solutes.at[:, dp, wide]),
                (gr.at[sp, slim], grains.at[dp, slim]),
            )
            pieces.append(group(pairs, dg, tt))
        return pieces

    main = [None]
    for src, size in ((0, SPLIT), (SPLIT, more - SPLIT)):
        sp, dp = pl.ds(src, size), pl.ds(own + src, size)
        pairs = (
            (ph.at[sp], PC.at[dp]),
            (so.at[:, sp], S0.at[pl.ds(4, 2), dp, pl.ds(OWN, rows)]),
            (gr.at[sp], GC.at[dp]),
        )
        main.append(group(pairs, -1, t))
    to_left = halo(PN, GN, SN, pl.ds(0, STEPS), pl.ds(0, STEPS - 1), left)
    to_right = halo(PL, GL, SL, pl.ds(rows - STEPS, STEPS), pl.ds(rows - STEPS + 1, STEPS - 1), right)

    inner = jnp.logical_not(first)
    outer = jnp.logical_not(last)

    def start_halo(copies):
        for copy in copies[0]:
            copy.start()

        @pl.when(inner)
        def _():
            for copy in copies[1] + copies[2]:
                copy.start()

    def start_far():
        @pl.when(far_left)
        def _():
            start_halo(to_left)

        @pl.when(far_right)
        def _():
            start_halo(to_right)

    def start_main():
        @pl.when(inner)
        def _():
            for copy in main[1] + main[2]:
                copy.start()

    def start_near():
        @pl.when(far_left)
        def _():
            start_halo(to_right)

        @pl.when(far_right)
        def _():
            start_halo(to_left)

        start_main()

    def meet():
        @pl.when(first)
        def _():
            pl.semaphore_wait(barrier, 2)

        @pl.when(inner)
        def _():
            pl.semaphore_wait(barrier, 5)

    @pl.when(jnp.logical_not(early))
    def _():
        meet()

        @pl.when(place == 1)
        def _():
            pl.semaphore_signal(ready, inc=1, device_id={"grow": g, "trans": left}, device_id_type=MESH)

        @pl.when(place == half - 2)
        def _():
            pl.semaphore_signal(ready, inc=1, device_id={"grow": g, "trans": right}, device_id_type=MESH)

        start_far()

    @pl.when(end)
    def _():
        pl.semaphore_wait(ready, 1)

    start_near()

    for copy in local[3:]:
        copy.wait()
    lane = lax.broadcasted_iota(jnp.int32, (rows, cols), 1)
    table = jnp.zeros((rows, cols), jnp.float32)
    for n in range(go.shape[0]):
        table = jnp.where(lane == n, om[go[n]] * TIME_STEP, table)
    TB[...] = table

    def expand(low, high, row, labels, grains, solutes):
        def body(w, _):
            at = pl.ds(row, rows)
            label = labels[w]
            for a in range(4):
                S0[a, w, at] = jnp.where(label == a, 1.0, 0.0)
            if solutes is not None:
                for k in range(2):
                    S0[4 + k, w, at] = solutes[k, w]
            grain = jnp.bitwise_and(grains[w], go.shape[0] - 1)
            mob = jnp.take_along_axis(TB[...], grain, axis=1)
            MO[w, at] = jnp.where(jnp.logical_and(last, w >= own), LIQUID_MOBILITY * TIME_STEP, mob)
            return 0

        lax.fori_loop(low, high, body, 0, unroll=2)

    part = [[pa[k, a] for k in range(2)] for a in range(4)]
    spread = (LIQUID_DIFFUSION - SOLID_DIFFUSION) * 0.5 * TIME_STEP
    base = SOLID_DIFFUSION * 0.5 * TIME_STEP

    def roll(v, shift):
        return pltpu.roll(v, shift % v.shape[1], 1)

    def cooling(height):
        return 2.0 * (0.5 - (height.astype(jnp.float32) + 0.5) / jnp.float32(n_grow * planes))

    def advance(load, w, up, down, undercool, mob):
        centre = [load(k, w, 0) for k in range(6)]
        above = [load(k, up, 0) for k in range(6)]
        below = [load(k, down, 0) for k in range(6)]
        rown = [load(k, w, 1) for k in range(6)]
        rowp = [load(k, w, -1) for k in range(6)]
        coln = [roll(v, -1) for v in centre]
        colp = [roll(v, 1) for v in centre[:4]]
        c0, c1 = centre[4], centre[5]
        forcing = []
        for a in range(4):
            p = centre[a]
            lap = ANISOTROPY * (above[a] + below[a]) + ((rown[a] + rowp[a]) + (coln[a] + colp[a])) - (2.0 * ANISOTROPY + 4.0) * p
            drive = (p + (COOLING_WEIGHTS[a] * undercool - 0.5)) + (FIRST_WEIGHTS[a] * c0 + SECOND_WEIGHTS[a] * c1)
            forcing.append(lap + (WELL_HEIGHT * p) * ((1.0 - p) * drive))
        mean = 0.25 * ((forcing[0] + forcing[1]) + (forcing[2] + forcing[3]))
        trials = [jnp.clip(centre[a] + mob * (forcing[a] - mean), 0.0, 1.0) for a in range(4)]
        scale = 1.0 / ((trials[0] + trials[1]) + (trials[2] + trials[3]))
        new = [v * scale for v in trials]
        changes = [new[a] - centre[a] for a in range(4)]
        own_d = 2.0 * base + spread * centre[0]
        sums = [None, None]
        d = own_d + spread * coln[0]
        for k in range(2):
            flow = d * (coln[4 + k] - centre[4 + k])
            sums[k] = flow - roll(flow, 1)
        for near in (above, below, rown, rowp):
            d = own_d + spread * near[0]
            for k in range(2):
                sums[k] = sums[k] + d * (near[4 + k] - centre[4 + k])
        for k in range(2):
            rejected = (part[0][k] * changes[0] + part[1][k] * changes[1]) + (part[2][k] * changes[2] + part[3][k] * changes[3])
            new.append((centre[4 + k] + sums[k]) - rejected)
        return new

    top = jnp.where(last, own - 1, length - 1)
    origin = g * planes + skip

    def one(low, high, row, size, unroll):
        def load(k, i, by):
            at = pl.ds(row + by, size)
            return S0[k, i, at]

        def body(w, _):
            new = advance(load, w, jnp.minimum(w + 1, top), w - 1, cooling(origin + w), MO[w, pl.ds(row, size)])
            for k in range(6):
                T1[k, w, pl.ds(row, size)] = new[k]
            return 0

        lax.fori_loop(low, high, body, 0, unroll=unroll)

    def two(low, high, row, size, unroll):
        def load(k, i, by):
            return T1[k, i, pl.ds(row + by, size)]

        def body(w, _):
            new = advance(load, w, jnp.minimum(w + 1, top), w - 1, cooling(origin + w), MO[w, pl.ds(row, size)])
            for k in range(6):
                T2[k, w, pl.ds(row, size)] = new[k]
            return 0

        lax.fori_loop(low, high, body, 0, unroll=unroll)

    bottom = jnp.where(first, STEPS, 0)

    def three(low, high, unroll):
        def load(k, i, by):
            return T2[k, i, pl.ds(OWN + by, rows)]

        def body(w, _):
            new = advance(load, w, w + 1, jnp.maximum(w - 1, bottom), cooling(g * planes + w - STEPS), MO[w, pl.ds(OWN, rows)])
            for k in range(4):
                pout[k, w - STEPS] = new[k]
            for k in range(2):
                sout[k, w - STEPS] = new[4 + k]
            return 0

        lax.fori_loop(low, high, body, 0, unroll=unroll)

    def flood(low, high):
        @pl.when(last)
        def _():
            def body(w, _):
                for k in range(6):
                    T2[k, w] = jnp.full((ROWS, cols), INFLOW[k], jnp.float32)
                return 0

            lax.fori_loop(max(low, own), high, body, 0)

    def arrive(copies):
        for copy in copies:
            copy.wait_recv()

    def take(pieces, before, near):
        low = (1, own, own + SPLIT)[pieces[0]]
        high = (own, own + SPLIT, length - 1)[pieces[-1]]

        def side(copies, row, buffers):
            def wait():
                for n in pieces:
                    arrive(copies[n])

            if pieces[0] == 0:
                wait()
            else:
                pl.when(outer)(wait)
            expand(low, high, row, *buffers)

        @pl.when(jnp.logical_and(before, far_left if near else far_right))
        def _():
            side(to_left, NEXT, (PN, GN, SN))

        @pl.when(jnp.logical_and(before, far_right if near else far_left))
        def _():
            side(to_right, 0, (PL, GL, SL))

    middle = jnp.logical_not(end)
    always = g >= 0
    wide = 2 * rows
    for copy in local[:3]:
        copy.wait()
    expand(0, own, OWN, PC, GC, None)

    @pl.when(sooner)
    def _():
        meet()
        start_far()

    take([0], always, True)
    take([0], middle, False)
    one(1, own - 1, OWN - 2, wide, UNROLL_WIDE)
    two(2, own - 2, OWN - 2, wide, UNROLL_WIDE)

    @pl.when(later)
    def _():
        meet()
        start_far()

    bounds = (1, own, own + SPLIT, length)

    def lows(n):
        return [max(bounds[n] - s, s) for s in (1, 2, 3)]

    def shut(n):
        if bounds[n + 1] - 2 > own:
            flood(lows(n)[1], bounds[n + 1] - 2)

    def finish(n):
        shut(n)
        three(lows(n)[2], bounds[n + 1] - 3, UNROLL_SLIM)

    finish(0)

    for n in (1, 2):

        @pl.when(outer)
        def _():
            arrive(main[n])

        expand(bounds[n], bounds[n + 1], OWN, PC, GC, None)
        take([n], always, True)
        take([n], middle, False)
        one(lows(n)[0], bounds[n + 1] - 1, OWN - 2, wide, UNROLL_WIDE)
        two(lows(n)[1], bounds[n + 1] - 2, OWN - 2, wide, UNROLL_WIDE)
        finish(n)

    quad = rows // 2
    upper = lax.broadcasted_iota(jnp.int32, (rows, cols), 0) < quad

    def pairs(low, high, source, row, above, below, height, store):
        def load(k, planes_of, by):
            ref = MO if k is None else source.at[k]
            return jnp.where(upper, ref[planes_of[0], pl.ds(row + by, rows)], ref[planes_of[1], pl.ds(row + by - quad, rows)])

        def body(n, _):
            w = low + 2 * n
            undercool = jnp.where(upper, cooling(height + w), cooling(height + w + 1))
            here = (w, w + 1)
            new = advance(load, here, (above(w), above(w + 1)), (below(w), below(w + 1)), undercool, load(None, here, 0))
            for k in range(6):
                store(k, w, new[k][:quad])
                store(k, w + 1, new[k][quad:])
            return 0

        count = (high - low + 1) // 2
        lax.fori_loop(0, count, body, 0, unroll=count)

    def keep(ref, row):
        def store(k, w, value):
            ref[k, w, pl.ds(row, quad)] = value

        return store

    def emit(k, w, value):
        at = pl.ds(jnp.where(far_right, quad, 0), quad)
        if k < 4:
            pout[k, w - STEPS, at] = value
        else:
            sout[k - 4, w - STEPS, at] = value

    rows_of = [jnp.where(far_right, NEXT + 2 - quad - s, OWN - 2 + s) for s in range(3)]

    def capped(w):
        return jnp.minimum(w + 1, top)

    for n in range(3):
        take([n], end, False)

        @pl.when(end)
        def _():
            low, high = lows(n), bounds[n + 1]
            pairs(low[0], high - 1, S0, rows_of[0], capped, lambda w: w - 1, origin, keep(T1, rows_of[0]))
            pairs(low[1], high - 2, T1, rows_of[1], capped, lambda w: w - 1, origin, keep(T2, rows_of[1]))
            shut(n)
            pairs(low[2], high - 3, T2, rows_of[2], lambda w: w + 1, lambda w: jnp.maximum(w - 1, bottom), g * planes - STEPS, emit)

    for copy in to_left[0] + to_right[0]:
        copy.wait_send()

    @pl.when(inner)
    def _():
        for copy in main[1] + main[2] + to_left[1] + to_left[2] + to_right[1] + to_right[2]:
            copy.wait_send()


def put_out(phases, solutes, pout, sout, done):
    pieces = [(phases.at[k], pout.at[k]) for k in range(4)] + [(solutes.at[k], sout.at[k]) for k in range(2)]
    copies = [pltpu.make_async_copy(src, dst, done.at[n]) for n, (src, dst) in enumerate(pieces)]
    for copy in copies:
        copy.start()
    for copy in copies:
        copy.wait()


def solution(mesh):
    n_grow, n_trans = mesh.shape["grow"], mesh.shape["trans"]

    def shards(phase_label, grain_label, grain_orient, orient_mobility, solute_init, partition):
        planes, rows, cols = phase_label.shape
        length = planes + 2 * STEPS
        window = (length, ROWS, cols)
        block = (length, rows, cols)
        hbm = pl.BlockSpec(memory_space=pl.ANY)
        vmem = pl.BlockSpec(memory_space=pltpu.VMEM)
        f32, i32 = jnp.float32, jnp.int32
        results = pl.pallas_call(
            functools.partial(kernel, n_grow, n_trans),
            out_shape=(
                pltpu.VMEM((4, planes, rows, cols), f32),
                pltpu.VMEM((2, planes, rows, cols), f32),
            ),
            in_specs=[hbm] * 6,
            out_specs=(vmem, vmem),
            scratch_shapes=[
                pltpu.VMEM(block, i32),
                pltpu.VMEM(block, i32),
                pltpu.VMEM(block, i32),
                pltpu.VMEM(block, i32),
                pltpu.VMEM((2, *block), f32),
                pltpu.VMEM(block, i32),
                pltpu.VMEM(block, i32),
                pltpu.VMEM((2, *block), f32),
                pltpu.VMEM((6, *window), f32),
                pltpu.VMEM(window, f32),
                pltpu.VMEM((6, *window), f32),
                pltpu.VMEM((6, *window), f32),
                pltpu.VMEM((rows, cols), f32),
                pltpu.SMEM(grain_orient.shape, i32),
                pltpu.SMEM(orient_mobility.shape, f32),
                pltpu.SMEM(partition.shape[::-1], f32),
                pltpu.SemaphoreType.DMA((6,)),
                pltpu.SemaphoreType.DMA((24,)),
                pltpu.SemaphoreType.DMA((24,)),
                pltpu.SemaphoreType.REGULAR,
            ],
            compiler_params=pltpu.CompilerParams(collective_id=0, has_side_effects=True),
        )(phase_label, grain_label, solute_init, grain_orient, orient_mobility, partition.T)
        return pl.pallas_call(
            put_out,
            out_shape=tuple(jax.ShapeDtypeStruct(r.shape, r.dtype) for r in results),
            in_specs=[vmem, vmem],
            out_specs=(hbm, hbm),
            scratch_shapes=[pltpu.SemaphoreType.DMA((PARTS,))],
        )(*[pltpu.with_memory_space_constraint(r, pltpu.VMEM) for r in results])

    placed = (P("grow", "trans", None), P("grow", "trans", None), P(), P(), P(None, "grow", "trans", None), P())
    return jax.shard_map(
        shards,
        mesh=mesh,
        in_specs=placed,
        out_specs=(P(None, "grow", "trans", None), P(None, "grow", "trans", None)),
        check_vma=False,
    )
```

```python
import functools

import jax
import jax.numpy as jnp
from jax import lax
from jax.experimental import pallas as pl
from jax.experimental.pallas import tpu as pltpu
from jax.sharding import PartitionSpec as P

MESH = pl.DeviceIdType.MESH
SHIFT = 16
STEPS = 3
ANISOTROPY = 1.5
WELL_HEIGHT = 4.0
TIME_STEP = 0.06
LIQUID_DIFFUSION = 1.0
SOLID_DIFFUSION = 0.1
COOLING_WEIGHTS = (-1.0, 0.8, 0.7, 0.6)
FIRST_WEIGHTS = (0.5, -1.0, 0.4, 0.3)
SECOND_WEIGHTS = (0.4, 0.3, -1.0, 0.5)
INFLOW = (1.0, 0.0, 0.0, 0.0, 0.3, 0.2)
LIQUID_MOBILITY = 1.0
ROWS, OWN, NEXT = 24, 8, 16
UNROLL_WIDE, UNROLL_SLIM = 3, 5
PARTS = 6
TURN = 8
SPLIT = 9


def kernel(n_grow, n_trans, ph, gr, so, go_h, om_h, pa_h, pout, sout, PC, GC, PL, GL, SL, PN, GN, SN, S0, MO, T1, T2, TB, go, om, pa, loc, send, recv, ready):
    g = lax.axis_index("grow")
    t = lax.axis_index("trans")
    planes, rows, cols = ph.shape
    left = lax.rem(t + n_trans - 1, n_trans)
    right = lax.rem(t + 1, n_trans)
    half = n_trans // 2
    place = lax.rem(t, half)
    first, last = g == 0, g == n_grow - 1
    far_right = place == half - 1
    far_left = jnp.logical_not(far_right)
    end = jnp.logical_or(place == 0, far_right)
    early = jnp.logical_and(end, t < half)
    sooner = jnp.logical_and(early, lax.rem(g, TURN) == 0)
    later = jnp.logical_and(early, lax.rem(g, TURN) != 0)
    own = planes - SHIFT + STEPS
    skip = planes - own
    more = SHIFT + STEPS
    length = own + more

    barrier = pltpu.get_barrier_semaphore()

    def greet(dg, tt):
        pl.semaphore_signal(barrier, inc=1, device_id={"grow": g + dg, "trans": tt}, device_id_type=MESH)

    greet(0, left)
    greet(0, right)

    @pl.when(jnp.logical_not(last))
    def _():
        greet(1, left)
        greet(1, right)
        greet(1, t)

    local = [
        pltpu.make_async_copy(src, dst, loc.at[n])
        for n, (src, dst) in enumerate(
            [
                (ph.at[pl.ds(skip, own)], PC.at[pl.ds(0, own)]),
                (gr.at[pl.ds(skip, own)], GC.at[pl.ds(0, own)]),
                (so.at[:, pl.ds(skip, own)], S0.at[pl.ds(4, 2), pl.ds(0, own), pl.ds(OWN, rows)]),
                (go_h, go),
                (om_h, om),
                (pa_h, pa),
            ]
        )
    ]
    for copy in local:
        copy.start()

    count = 0

    def group(pairs, dg, tt):
        nonlocal count
        copies = []
        for src, dst in pairs:
            copies.append(
                pltpu.make_async_remote_copy(
                    src_ref=src,
                    dst_ref=dst,
                    send_sem=send.at[count],
                    recv_sem=recv.at[count],
                    device_id={"grow": g + dg, "trans": tt},
                    device_id_type=MESH,
                )
            )
            count += 1
        return copies

    def halo(labels, grains, solutes, wide, slim, tt):
        pieces = []
        for src, size, dst, dg in (
            (skip + 1, own - 1, 1, 0),
            (0, SPLIT, own, -1),
            (SPLIT, more - 1 - SPLIT, own + SPLIT, -1),
        ):
            sp, dp = pl.ds(src, size), pl.ds(dst, size)
            pairs = (
                (ph.at[sp, wide], labels.at[dp, wide]),
                (so.at[:, sp, wide], solutes.at[:, dp, wide]),
                (gr.at[sp, slim], grains.at[dp, slim]),
            )
            pieces.append(group(pairs, dg, tt))
        return pieces

    main = [None]
    for src, size in ((0, SPLIT), (SPLIT, more - SPLIT)):
        sp, dp = pl.ds(src, size), pl.ds(own + src, size)
        pairs = (
            (ph.at[sp], PC.at[dp]),
            (so.at[:, sp], S0.at[pl.ds(4, 2), dp, pl.ds(OWN, rows)]),
            (gr.at[sp], GC.at[dp]),
        )
        main.append(group(pairs, -1, t))
    to_left = halo(PN, GN, SN, pl.ds(0, STEPS), pl.ds(0, STEPS - 1), left)
    to_right = halo(PL, GL, SL, pl.ds(rows - STEPS, STEPS), pl.ds(rows - STEPS + 1, STEPS - 1), right)

    inner = jnp.logical_not(first)
    outer = jnp.logical_not(last)

    def start_halo(copies):
        for copy in copies[0]:
            copy.start()

        @pl.when(inner)
        def _():
            for copy in copies[1] + copies[2]:
                copy.start()

    def start_far():
        @pl.when(far_left)
        def _():
            start_halo(to_left)

        @pl.when(far_right)
        def _():
            start_halo(to_right)

    def start_main():
        @pl.when(inner)
        def _():
            for copy in main[1] + main[2]:
                copy.start()

    def start_near():
        start_main()

        @pl.when(far_left)
        def _():
            start_halo(to_right)

        @pl.when(far_right)
        def _():
            start_halo(to_left)


    def meet():
        @pl.when(first)
        def _():
            pl.semaphore_wait(barrier, 2)

        @pl.when(inner)
        def _():
            pl.semaphore_wait(barrier, 5)

    @pl.when(jnp.logical_not(early))
    def _():
        meet()

        @pl.when(place == 1)
        def _():
            pl.semaphore_signal(ready, inc=1, device_id={"grow": g, "trans": left}, device_id_type=MESH)

        @pl.when(place == half - 2)
        def _():
            pl.semaphore_signal(ready, inc=1, device_id={"grow": g, "trans": right}, device_id_type=MESH)

        start_far()

    @pl.when(end)
    def _():
        pl.semaphore_wait(ready, 1)

    start_near()

    for copy in local[3:]:
        copy.wait()
    lane = lax.broadcasted_iota(jnp.int32, (rows, cols), 1)
    table = jnp.zeros((rows, cols), jnp.float32)
    for n in range(go.shape[0]):
        table = jnp.where(lane == n, om[go[n]] * TIME_STEP, table)
    TB[...] = table

    def expand(low, high, row, labels, grains, solutes):
        def body(w, _):
            at = pl.ds(row, rows)
            label = labels[w]
            for a in range(4):
                S0[a, w, at] = jnp.where(label == a, 1.0, 0.0)
            if solutes is not None:
                for k in range(2):
                    S0[4 + k, w, at] = solutes[k, w]
            grain = jnp.bitwise_and(grains[w], go.shape[0] - 1)
            mob = jnp.take_along_axis(TB[...], grain, axis=1)
            MO[w, at] = jnp.where(jnp.logical_and(last, w >= own), LIQUID_MOBILITY * TIME_STEP, mob)
            return 0

        lax.fori_loop(low, high, body, 0, unroll=2)

    part = [[pa[k, a] for k in range(2)] for a in range(4)]
    spread = (LIQUID_DIFFUSION - SOLID_DIFFUSION) * 0.5 * TIME_STEP
    base = SOLID_DIFFUSION * 0.5 * TIME_STEP

    def roll(v, shift):
        return pltpu.roll(v, shift % v.shape[1], 1)

    def cooling(height):
        return 2.0 * (0.5 - (height.astype(jnp.float32) + 0.5) / jnp.float32(n_grow * planes))

    def advance(load, w, up, down, undercool, mob):
        centre = [load(k, w, 0) for k in range(6)]
        above = [load(k, up, 0) for k in range(6)]
        below = [load(k, down, 0) for k in range(6)]
        rown = [load(k, w, 1) for k in range(6)]
        rowp = [load(k, w, -1) for k in range(6)]
        coln = [roll(v, -1) for v in centre]
        colp = [roll(v, 1) for v in centre[:4]]
        c0, c1 = centre[4], centre[5]
        forcing = []
        for a in range(4):
            p = centre[a]
            lap = ANISOTROPY * (above[a] + below[a]) + ((rown[a] + rowp[a]) + (coln[a] + colp[a])) - (2.0 * ANISOTROPY + 4.0) * p
            drive = (p + (COOLING_WEIGHTS[a] * undercool - 0.5)) + (FIRST_WEIGHTS[a] * c0 + SECOND_WEIGHTS[a] * c1)
            forcing.append(lap + (WELL_HEIGHT * p) * ((1.0 - p) * drive))
        mean = 0.25 * ((forcing[0] + forcing[1]) + (forcing[2] + forcing[3]))
        trials = [jnp.clip(centre[a] + mob * (forcing[a] - mean), 0.0, 1.0) for a in range(4)]
        scale = 1.0 / ((trials[0] + trials[1]) + (trials[2] + trials[3]))
        new = [v * scale for v in trials]
        changes = [new[a] - centre[a] for a in range(4)]
        own_d = 2.0 * base + spread * centre[0]
        sums = [None, None]
        d = own_d + spread * coln[0]
        for k in range(2):
            flow = d * (coln[4 + k] - centre[4 + k])
            sums[k] = flow - roll(flow, 1)
        for near in (above, below, rown, rowp):
            d = own_d + spread * near[0]
            for k in range(2):
                sums[k] = sums[k] + d * (near[4 + k] - centre[4 + k])
        for k in range(2):
            rejected = (part[0][k] * changes[0] + part[1][k] * changes[1]) + (part[2][k] * changes[2] + part[3][k] * changes[3])
            new.append((centre[4 + k] + sums[k]) - rejected)
        return new

    top = jnp.where(last, own - 1, length - 1)
    origin = g * planes + skip

    def one(low, high, row, size, unroll):
        def load(k, i, by):
            at = pl.ds(row + by, size)
            return S0[k, i, at]

        def body(w, _):
            new = advance(load, w, jnp.minimum(w + 1, top), w - 1, cooling(origin + w), MO[w, pl.ds(row, size)])
            for k in range(6):
                T1[k, w, pl.ds(row, size)] = new[k]
            return 0

        lax.fori_loop(low, high, body, 0, unroll=unroll)

    def two(low, high, row, size, unroll):
        def load(k, i, by):
            return T1[k, i, pl.ds(row + by, size)]

        def body(w, _):
            new = advance(load, w, jnp.minimum(w + 1, top), w - 1, cooling(origin + w), MO[w, pl.ds(row, size)])
            for k in range(6):
                T2[k, w, pl.ds(row, size)] = new[k]
            return 0

        lax.fori_loop(low, high, body, 0, unroll=unroll)

    bottom = jnp.where(first, STEPS, 0)

    def three(low, high, unroll):
        def load(k, i, by):
            return T2[k, i, pl.ds(OWN + by, rows)]

        def body(w, _):
            new = advance(load, w, w + 1, jnp.maximum(w - 1, bottom), cooling(g * planes + w - STEPS), MO[w, pl.ds(OWN, rows)])
            for k in range(4):
                pout[k, w - STEPS] = new[k]
            for k in range(2):
                sout[k, w - STEPS] = new[4 + k]
            return 0

        lax.fori_loop(low, high, body, 0, unroll=unroll)

    def flood(low, high):
        @pl.when(last)
        def _():
            def body(w, _):
                for k in range(6):
                    T2[k, w] = jnp.full((ROWS, cols), INFLOW[k], jnp.float32)
                return 0

            lax.fori_loop(max(low, own), high, body, 0)

    def arrive(copies):
        for copy in copies:
            copy.wait_recv()

    def take(pieces, before, near):
        low = (1, own, own + SPLIT)[pieces[0]]
        high = (own, own + SPLIT, length - 1)[pieces[-1]]

        def side(copies, row, buffers):
            def wait():
                for n in pieces:
                    arrive(copies[n])

            if pieces[0] == 0:
                wait()
            else:
                pl.when(outer)(wait)
            expand(low, high, row, *buffers)

        @pl.when(jnp.logical_and(before, far_left if near else far_right))
        def _():
            side(to_left, NEXT, (PN, GN, SN))

        @pl.when(jnp.logical_and(before, far_right if near else far_left))
        def _():
            side(to_right, 0, (PL, GL, SL))

    middle = jnp.logical_not(end)
    always = g >= 0
    wide = 2 * rows
    for copy in local[:3]:
        copy.wait()
    expand(0, own, OWN, PC, GC, None)

    @pl.when(sooner)
    def _():
        meet()
        start_far()

    take([0], always, True)
    take([0], middle, False)
    one(1, own - 1, OWN - 2, wide, UNROLL_WIDE)
    two(2, own - 2, OWN - 2, wide, UNROLL_WIDE)

    @pl.when(later)
    def _():
        meet()
        start_far()

    bounds = (1, own, own + SPLIT, length)

    def lows(n):
        return [max(bounds[n] - s, s) for s in (1, 2, 3)]

    def shut(n):
        if bounds[n + 1] - 2 > own:
            flood(lows(n)[1], bounds[n + 1] - 2)

    def finish(n):
        shut(n)
        three(lows(n)[2], bounds[n + 1] - 3, UNROLL_SLIM)

    finish(0)

    for n in (1, 2):

        @pl.when(outer)
        def _():
            arrive(main[n])

        expand(bounds[n], bounds[n + 1], OWN, PC, GC, None)
        take([n], always, True)
        take([n], middle, False)
        one(lows(n)[0], bounds[n + 1] - 1, OWN - 2, wide, UNROLL_WIDE)
        two(lows(n)[1], bounds[n + 1] - 2, OWN - 2, wide, UNROLL_WIDE)
        finish(n)

    quad = rows // 2
    upper = lax.broadcasted_iota(jnp.int32, (rows, cols), 0) < quad

    def pairs(low, high, source, row, above, below, height, store):
        def load(k, planes_of, by):
            ref = MO if k is None else source.at[k]
            return jnp.where(upper, ref[planes_of[0], pl.ds(row + by, rows)], ref[planes_of[1], pl.ds(row + by - quad, rows)])

        def body(n, _):
            w = low + 2 * n
            undercool = jnp.where(upper, cooling(height + w), cooling(height + w + 1))
            here = (w, w + 1)
            new = advance(load, here, (above(w), above(w + 1)), (below(w), below(w + 1)), undercool, load(None, here, 0))
            for k in range(6):
                store(k, w, new[k][:quad])
                store(k, w + 1, new[k][quad:])
            return 0

        count = (high - low + 1) // 2
        lax.fori_loop(0, count, body, 0, unroll=count)

    def keep(ref, row):
        def store(k, w, value):
            ref[k, w, pl.ds(row, quad)] = value

        return store

    def emit(k, w, value):
        at = pl.ds(jnp.where(far_right, quad, 0), quad)
        if k < 4:
            pout[k, w - STEPS, at] = value
        else:
            sout[k - 4, w - STEPS, at] = value

    rows_of = [jnp.where(far_right, NEXT + 2 - quad - s, OWN - 2 + s) for s in range(3)]

    def capped(w):
        return jnp.minimum(w + 1, top)

    for n in range(3):
        take([n], end, False)

        @pl.when(end)
        def _():
            low, high = lows(n), bounds[n + 1]
            pairs(low[0], high - 1, S0, rows_of[0], capped, lambda w: w - 1, origin, keep(T1, rows_of[0]))
            pairs(low[1], high - 2, T1, rows_of[1], capped, lambda w: w - 1, origin, keep(T2, rows_of[1]))
            shut(n)
            pairs(low[2], high - 3, T2, rows_of[2], lambda w: w + 1, lambda w: jnp.maximum(w - 1, bottom), g * planes - STEPS, emit)

    for copy in to_left[0] + to_right[0]:
        copy.wait_send()

    @pl.when(inner)
    def _():
        for copy in main[1] + main[2] + to_left[1] + to_left[2] + to_right[1] + to_right[2]:
            copy.wait_send()


def put_out(phases, solutes, pout, sout, done):
    pieces = [(phases.at[k], pout.at[k]) for k in range(4)] + [(solutes.at[k], sout.at[k]) for k in range(2)]
    copies = [pltpu.make_async_copy(src, dst, done.at[n]) for n, (src, dst) in enumerate(pieces)]
    for copy in copies:
        copy.start()
    for copy in copies:
        copy.wait()


def solution(mesh):
    n_grow, n_trans = mesh.shape["grow"], mesh.shape["trans"]

    def shards(phase_label, grain_label, grain_orient, orient_mobility, solute_init, partition):
        planes, rows, cols = phase_label.shape
        length = planes + 2 * STEPS
        window = (length, ROWS, cols)
        block = (length, rows, cols)
        hbm = pl.BlockSpec(memory_space=pl.ANY)
        vmem = pl.BlockSpec(memory_space=pltpu.VMEM)
        f32, i32 = jnp.float32, jnp.int32
        results = pl.pallas_call(
            functools.partial(kernel, n_grow, n_trans),
            out_shape=(
                pltpu.VMEM((4, planes, rows, cols), f32),
                pltpu.VMEM((2, planes, rows, cols), f32),
            ),
            in_specs=[hbm] * 6,
            out_specs=(vmem, vmem),
            scratch_shapes=[
                pltpu.VMEM(block, i32),
                pltpu.VMEM(block, i32),
                pltpu.VMEM(block, i32),
                pltpu.VMEM(block, i32),
                pltpu.VMEM((2, *block), f32),
                pltpu.VMEM(block, i32),
                pltpu.VMEM(block, i32),
                pltpu.VMEM((2, *block), f32),
                pltpu.VMEM((6, *window), f32),
                pltpu.VMEM(window, f32),
                pltpu.VMEM((6, *window), f32),
                pltpu.VMEM((6, *window), f32),
                pltpu.VMEM((rows, cols), f32),
                pltpu.SMEM(grain_orient.shape, i32),
                pltpu.SMEM(orient_mobility.shape, f32),
                pltpu.SMEM(partition.shape[::-1], f32),
                pltpu.SemaphoreType.DMA((6,)),
                pltpu.SemaphoreType.DMA((24,)),
                pltpu.SemaphoreType.DMA((24,)),
                pltpu.SemaphoreType.REGULAR,
            ],
            compiler_params=pltpu.CompilerParams(collective_id=0, has_side_effects=True),
        )(phase_label, grain_label, solute_init, grain_orient, orient_mobility, partition.T)
        return pl.pallas_call(
            put_out,
            out_shape=tuple(jax.ShapeDtypeStruct(r.shape, r.dtype) for r in results),
            in_specs=[vmem, vmem],
            out_specs=(hbm, hbm),
            scratch_shapes=[pltpu.SemaphoreType.DMA((PARTS,))],
        )(*[pltpu.with_memory_space_constraint(r, pltpu.VMEM) for r in results])

    placed = (P("grow", "trans", None), P("grow", "trans", None), P(), P(), P(None, "grow", "trans", None), P())
    return jax.shard_map(
        shards,
        mesh=mesh,
        in_specs=placed,
        out_specs=(P(None, "grow", "trans", None), P(None, "grow", "trans", None)),
        check_vma=False,
    )
```
